512 devices in a mesh: kz: 16 (over x, z_hi), gx: 32 (over y, z_lo, core).
Axes of the slice: x: 4, y: 8, z: 8 (z_hi: 4, z_lo: 2; z = z_hi * 2 + z_lo), core: 2. Of those that a mesh axis runs over, the one named last changes fastest.
Arguments:
- kspace_lines: bfloat16 [16, 16, 128, 2, 512], P(None, 'kz', 'gx'), may hold values from -6 to 6
- acquired_at: int32 [16, 128], P('kz'), may hold values from 0 to 5
- ky_start: int32 [6], replicated, may hold values from -2 to 0, as said below
- kz_start: int32 [6], replicated, may hold values from -1 to 0, as said below
- kernels: bfloat16 [2, 6, 16, 6, 32], replicated, may hold values from -0.3125 to 0.3125
Outputs:
- filled: bfloat16 [2, 512, 16, 32, 384], P(None, 'gx', None, 'kz')
The draws below stay inside these ranges and needn't reach their ends.
Inputs may be any that keep to these rules, and one draw needn't show every extreme that they name: acquired_at[b, a] = 2 ry + rz names the acquired position of the cell, with ky = 3 a + ry and kz = 2 b + rz. `ky_start`: each of -2, -1 and 0 appears exactly twice. `kz_start`: each of -1 and 0 appears exactly three times.
All inputs are finite; a program needn't handle non-finite values.
Results may differ from the reference program's by a relative error of at most 0.0057.
Values may be sent and summed in bfloat16 or wider, within the bound.
No kernel may reach another device: no remote copies, remote signals or barrier semaphores. Data moves between devices by JAX's collectives and lax.ppermute only.
A program may use at most 64 MiB of HBM per device.

```python
import math
import jax
import jax.numpy as jnp
from jax import lax

COILS = 16
NX = 512
NZC = 16
NY3 = 128
NZ = 32
NY = 384


def draw_ky_start(key, part):
    return (jax.random.permutation(key, 6) % 3 - 2).astype(jnp.int32)


def draw_kz_start(key, part):
    return (jax.random.permutation(jax.random.fold_in(key, 7), 6) % 2 - 1).astype(jnp.int32)


def place_ends(values, stream_key, least, high):
    longest = values.shape.index(max(values.shape))
    spots = []
    for shift in (0, 1):
        where = [jax.random.randint(jax.random.fold_in(stream_key, axis), (), 0, length) for axis, length in enumerate(values.shape)]
        where[longest] = (where[longest] + shift) % values.shape[longest]
        spots.append(tuple(where))
    return values.at[spots[0]].set(least).at[spots[1]].set(high)


def steps_of(stream_key, shape, cuts, least, top_value):
    loudness = 1.0
    for dim, shards_of in cuts:
        draws = jax.random.uniform(jax.random.fold_in(jax.random.fold_in(stream_key, 6), dim), (shards_of,), jnp.float32, least / len(cuts), top_value / len(cuts))
        loudness = loudness * jnp.repeat(jnp.exp(draws), shape[dim] // shards_of).reshape((-1,) + (1,) * (len(shape) - 1 - dim))
    return loudness


def bell_draw(rng, dims, deviation, most, shards=(), kind=jnp.bfloat16):
    values = deviation * jax.random.normal(rng, dims, jnp.float32)
    if shards:
        values = values * steps_of(rng, dims, shards, -0.22, 0.18)
    return jnp.clip(values, -most, most).astype(kind)


def setup_inputs(seed: int = 0) -> dict:
    keys = jax.random.split(jax.random.key(seed), 6)
    kspace_lines = bell_draw(keys[0], (COILS, NZC, NY3, 2, NX), 1.0, 6.0, ((1, 16), (2, 32)))
    acquired_at = place_ends(jax.random.randint(keys[1], (NZC, NY3), 0, 6), jax.random.fold_in(keys[1], 1), 0, 5).astype(jnp.int32)
    ky_start = draw_ky_start(jax.random.fold_in(keys[5], 71), 0)
    kz_start = draw_kz_start(jax.random.fold_in(keys[5], 71), 0)
    kernels = bell_draw(keys[4], (2, 6, COILS, 6, 2 * COILS), (24 * COILS) ** -0.5, 0.3125)
    return dict(kspace_lines=kspace_lines, acquired_at=acquired_at, ky_start=ky_start, kz_start=kz_start, kernels=kernels)


def readout_matrix(extent):
    wave_index = jnp.arange(extent, dtype=jnp.int32)
    phase_angle = (wave_index[:, None] * wave_index[None, :] % extent).astype(jnp.float32) * (2.0 * math.pi / extent)
    cosine = jnp.cos(phase_angle) / math.sqrt(extent)
    sine_part = jnp.sin(phase_angle) / math.sqrt(extent)
    from_real = jnp.stack([cosine, sine_part], axis=1)
    from_imag = jnp.stack([-sine_part, cosine], axis=1)
    return jnp.stack([from_real, from_imag], axis=0).astype(jnp.bfloat16)

def conjugate_flip(blocks):
    flipped = blocks[:, :, :, ::-1, ::-1]
    return jnp.concatenate([flipped[0:1], -flipped[1:2]], axis=0)

def complex_weights(kernels):
    real_part = kernels[0]
    imag_part = kernels[1]
    to_real = jnp.stack([real_part, -imag_part], axis=3)
    to_imag = jnp.stack([imag_part, real_part], axis=3)
    return jnp.stack([to_real, to_imag], axis=1)

def fill_grid(padded, actual, weights, acquired_at, ky_start, kz_start):
    kz_cells = actual.shape[3]
    ky_cells = actual.shape[4]
    filled = []
    for target in range(6):
        pieces = []
        for kz_point in range(2):
            kz_from = (kz_start[target] + 1 + kz_point).astype(jnp.int32)
            plane_rows = lax.dynamic_slice_in_dim(padded, kz_from, kz_cells, axis=3)
            for ky_point in range(3):
                ky_from = (ky_start[target] + 2 + ky_point).astype(jnp.int32)
                pieces.append(lax.dynamic_slice_in_dim(plane_rows, ky_from, ky_cells, axis=4))
        source = jnp.stack(pieces, axis=0).astype(jnp.float32)
        estimate = jnp.einsum('scpqh,pqxhba->sxcba', weights[target].astype(jnp.float32), source)
        chosen = jnp.where(acquired_at == target, actual.astype(jnp.float32), estimate)
        filled.append(chosen.astype(jnp.bfloat16))
    stacked = jnp.stack(filled, axis=0).reshape((3, 2) + actual.shape)
    reordered = jnp.transpose(stacked, (2, 3, 4, 5, 1, 6, 0))
    return reordered.reshape(actual.shape[0], actual.shape[1], actual.shape[2], 2 * kz_cells, 3 * ky_cells)

def reference(kspace_lines, acquired_at, ky_start, kz_start, kernels):
    spectra = jnp.einsum('cbaqk,qksx->sxcba', kspace_lines.astype(jnp.float32), readout_matrix(NX).astype(jnp.float32)).astype(jnp.bfloat16)
    channels = jnp.concatenate([spectra, conjugate_flip(spectra)], axis=2)
    padded = jnp.pad(channels, ((0, 0), (0, 0), (0, 0), (1, 1), (2, 2)))
    weights = complex_weights(kernels)
    block_width = math.gcd(NX, 16)
    groups = NX // block_width

    def split_x(values):
        return jnp.moveaxis(values.reshape((2, groups, block_width) + values.shape[2:]), 1, 0)

    def one_group(operands):
        return fill_grid(operands[0], operands[1], weights, acquired_at, ky_start, kz_start)
    result = lax.map(one_group, (split_x(padded), split_x(spectra)))
    return jnp.moveaxis(result, 0, 1).reshape(2, NX, COILS, NZ, NY)
```

```python
import math

import jax
import jax.numpy as jnp
import numpy as np
from jax import lax
from jax.experimental import pallas as pl
from jax.experimental.pallas import tpu as pltpu
from jax.sharding import PartitionSpec as P

COILS = 16
NX = 512
NZC = 16
NY3 = 128
GX = 32
AL = NY3 // GX
NXL = NX // GX
SC = 2 * COILS
SHIFTS = 5
ROWS3 = 3
KDIM = ROWS3 * SHIFTS * 2 * SC
F32 = jnp.float32
BF16 = jnp.bfloat16


def dft_table():
    index = np.arange(NX)
    angle = (index[:, None] * index[None, :] % NX) * (2.0 * math.pi / NX)
    table = np.concatenate([np.cos(angle), np.sin(angle)], axis=1) / math.sqrt(NX)
    return jnp.asarray(table.astype(np.float32)).astype(BF16)


def iota(shape, dim):
    return lax.broadcasted_iota(jnp.int32, shape, dim)


def onehot(condition):
    return jnp.where(condition, 1.0, 0.0).astype(BF16)


def dot(a, b):
    return lax.dot_general(a, b, (((1,), (0,)), ((), ())), preferred_element_type=F32)


def dot_t(a, b):
    return lax.dot_general(a, b, (((1,), (1,)), ((), ())), preferred_element_type=F32)


def dft_kernel(lines_ref, table_ref, out_ref):
    lines = lines_ref[...].reshape(COILS * AL * 2, NX)
    size = COILS * AL * 2
    row, col = iota((size, size), 0), iota((size, size), 1)
    al, s, c = row // SC, (row // COILS) % 2, row % COILS
    line = (c * AL + al) * 2
    same = onehot(col == line + s)
    cross = onehot(col == line + 1 - s)
    cross = jnp.where(s == 0, -cross.astype(F32), cross.astype(F32)).astype(BF16)
    direct = dot(same, lines).astype(BF16)
    crossed = dot(cross, lines).astype(BF16)
    both = jnp.concatenate([direct, crossed], axis=1)
    spectra = dot_t(table_ref[...], both)
    out_ref[...] = spectra.astype(BF16).reshape(GX, NXL, size)


def dft(lines):
    return pl.pallas_call(
        dft_kernel,
        out_shape=jax.ShapeDtypeStruct((GX, NXL, COILS * AL * 2), BF16),
        name="dft",
    )(lines, dft_table())


def slab_kernel(in_ref, out_ref):
    value = in_ref[...].reshape(GX * NXL, AL * SC)
    size = GX * NXL
    row, col = iota((size, size), 0), iota((size, size), 1)
    order = onehot(col == (row % GX) * NXL + row // GX)
    rows = dot(order, value).astype(BF16)
    eye = onehot(iota((128, 128), 0) == iota((128, 128), 1))
    group = 128 // GX
    wide = AL * 128
    kk, nn = iota((wide, group * NY3), 0), iota((wide, group * NY3), 1)
    place = onehot(
        (kk % 128) // GX * NY3 + (kk % GX) * AL + kk // 128 == nn
    )
    for part in range(NXL // group):
        turned = dot_t(eye, rows[part * 128 : (part + 1) * 128]).astype(BF16)
        flat = jnp.concatenate(
            [turned[al * SC : (al + 1) * SC] for al in range(AL)], axis=1
        )
        spread = dot(flat, place).astype(BF16)
        for x in range(group):
            out_ref[part * group + x] = spread[:, x * NY3 : (x + 1) * NY3]


def to_slab(lines):
    return pl.pallas_call(
        slab_kernel,
        out_shape=jax.ShapeDtypeStruct((NXL, SC, NY3), BF16),
        name="slab",
    )(lines)


def fill_kernel(
    a0_ref, a1_ref, a2_ref, v0_ref, v1_ref, v2_ref, weight_ref, acquired_ref,
    out_ref, source_ref,
):
    lane_in = iota((NY3, SHIFTS * NY3), 0)
    lane_out = iota((NY3, SHIFTS * NY3), 1)
    want = lane_out % NY3 + lane_out // NY3 - 2
    straight = onehot(lane_in == want)
    mirrored = onehot(NY3 - 1 - lane_in == want)
    slabs = ((a0_ref, a1_ref, a2_ref, straight), (v0_ref, v1_ref, v2_ref, mirrored))
    for v in range(2):
        for rho in range(ROWS3):
            slab = slabs[v][rho][...].reshape(NXL * SC, NY3)
            moved = dot(slab, slabs[v][3]).astype(BF16)
            for d in range(SHIFTS):
                at = ((rho * SHIFTS + d) * 2 + v) * SC
                for x in range(NXL):
                    source_ref[x // 2, at : at + SC, (x % 2) * NY3 : (x % 2 + 1) * NY3] = moved[
                        x * SC : (x + 1) * SC, d * NY3 : (d + 1) * NY3
                    ]
    weights = weight_ref[...]
    acquired = acquired_ref[...]
    kk, nn = iota((3 * NY3, 3 * NY3), 0), iota((3 * NY3, 3 * NY3), 1)
    weave = onehot((kk % NY3) * 3 + kk // NY3 == nn)
    parity = iota((2 * SC, NY3), 0) % 2
    masks = [jnp.broadcast_to(acquired, (2 * SC, NY3)) == 2 * ry + parity for ry in range(3)]
    for pair in range(NXL // 2):
        result = dot(weights, source_ref[pair])
        for half in range(2):
            x = 2 * pair + half
            lanes = slice(half * NY3, (half + 1) * NY3)
            kept = result[6 * SC : 8 * SC, lanes]
            chosen = [
                jnp.where(masks[ry], kept, result[ry * 2 * SC : (ry + 1) * 2 * SC, lanes])
                for ry in range(3)
            ]
            line = jnp.concatenate(chosen, axis=1).astype(BF16)
            woven = dot(line, weave).astype(BF16)
            for s in range(2):
                out_ref[s, x] = woven[s * SC : (s + 1) * SC].reshape(COILS, 2, 3 * NY3)


def fill(slabs, weights, acquired_at):
    return pl.pallas_call(
        fill_kernel,
        out_shape=jax.ShapeDtypeStruct((2, NXL, COILS, 2, 3 * NY3), BF16),
        scratch_shapes=[pltpu.VMEM((NXL // 2, KDIM, 2 * NY3), BF16)],
        name="fill",
    )(*slabs, weights, acquired_at)


def placed_weights(kernels, ky_start, kz_start):
    real = kernels[0].reshape(6, COILS, 6, 2, COILS)
    imag = kernels[1].reshape(6, COILS, 6, 2, COILS)
    sign = jnp.asarray([1.0, -1.0], BF16)[:, None]
    to_real = jnp.stack([real, -imag * sign], axis=4)
    to_imag = jnp.stack([imag, real * sign], axis=4)
    parts = jnp.stack([to_real, to_imag], axis=1).reshape(6, 2, COILS, 6, 2 * SC)
    spot = jnp.arange(ROWS3 * SHIFTS, dtype=jnp.int32)
    placed = 0
    for j in range(2):
        for i in range(3):
            target = (kz_start + 1 + j) * SHIFTS + ky_start + 2 + i
            here = (target[:, None] == spot[None, :])[:, None, None, :, None]
            placed = placed + jnp.where(here, parts[:, :, :, 3 * j + i, None, :], jnp.zeros((), BF16))
    placed = placed.reshape(3, 2, 2, COILS, KDIM).transpose(0, 2, 3, 1, 4).reshape(6 * SC, KDIM)
    own = np.zeros((SC, 2, KDIM), np.float32)
    for sc in range(SC):
        own[sc, :, ((1 * SHIFTS + 2) * 2) * SC + sc] = 1.0
    own = jnp.asarray(own.reshape(2 * SC, KDIM)).astype(BF16)
    return jnp.concatenate([placed, own], axis=0)


def local(kspace_lines, acquired_at, ky_start, kz_start, kernels):
    spectra = dft(kspace_lines)
    gathered = lax.all_to_all(spectra, "gx", split_axis=0, concat_axis=0, tiled=True)
    own = to_slab(gathered)

    def fetch(offset_of):
        pairs = [(offset_of(b), b) for b in range(NZC) if 0 <= offset_of(b) < NZC]
        return lax.ppermute(own, "kz", pairs)

    below = fetch(lambda b: b - 1)
    above = fetch(lambda b: b + 1)
    mirror = fetch(lambda b: NZC - 1 - b)
    mirror_below = fetch(lambda b: NZC - b)
    mirror_above = fetch(lambda b: NZC - 2 - b)
    weights = placed_weights(kernels, ky_start, kz_start)
    return fill(
        (below, own, above, mirror_below, mirror, mirror_above), weights, acquired_at
    )


def solution(mesh):
    placed = (P(None, "kz", "gx", None, None), P("kz", None), P(), P(), P())
    return jax.shard_map(
        local,
        mesh=mesh,
        in_specs=placed,
        out_specs=P(None, "gx", None, "kz", None),
        check_vma=False,
    )
```

```python
import math

import jax
import jax.numpy as jnp
import numpy as np
from jax import lax
from jax.experimental import pallas as pl
from jax.experimental.pallas import tpu as pltpu
from jax.sharding import PartitionSpec as P

COILS = 16
NX = 512
NZC = 16
NY3 = 128
GX = 32
AL = NY3 // GX
NXL = NX // GX
SC = 2 * COILS
SHIFTS = 5
ROWS3 = 3
KDIM = ROWS3 * SHIFTS * 2 * SC
KPAD = 1024
F32 = jnp.float32
BF16 = jnp.bfloat16


def dft_table():
    index = np.arange(NX // 2)
    angle = (index[:, None] * index[None, :] % NX) * (2.0 * math.pi / NX)
    table = np.concatenate([np.cos(angle), np.sin(angle)], axis=1) / math.sqrt(NX)
    return jnp.asarray(table.astype(np.float32)).astype(BF16)


def iota(shape, dim):
    return lax.broadcasted_iota(jnp.int32, shape, dim)


def onehot(condition):
    return jnp.where(condition, 1.0, 0.0).astype(BF16)


def dot(a, b):
    return lax.dot_general(a, b, (((1,), (0,)), ((), ())), preferred_element_type=F32)


def dot_t(a, b):
    return lax.dot_general(a, b, (((1,), (1,)), ((), ())), preferred_element_type=F32)


def room(mib):
    return pltpu.CompilerParams(vmem_limit_bytes=mib << 20)


def column_onehot(target, lanes):
    return onehot(target == iota((target.shape[0], lanes), 1))


def dft_kernel(lines_hbm, table_hbm, out_ref, lines_ref, table_ref, sems):
    lines_copy = pltpu.make_async_copy(lines_hbm, lines_ref, sems.at[0])
    table_copy = pltpu.make_async_copy(table_hbm, table_ref, sems.at[1])
    lines_copy.start()
    table_copy.start()
    size = COILS * AL * 2
    row = iota((size, 1), 0)
    al, s, c = row // SC, (row // COILS) % 2, row % COILS
    line = (c * AL + al) * 2
    same = column_onehot(line + s, size)
    cross = column_onehot(line + 1 - s, size).astype(F32)
    cross = jnp.where(s == 0, -cross, cross).astype(BF16)
    lines_copy.wait()
    lines = lines_ref[...].reshape(size, NX)
    direct = dot(same, lines)
    crossed = dot(cross, lines)
    half = NX // 2
    flip = iota((size, half), 1) % 2 == 0
    parts = [
        jnp.concatenate([direct[:, lanes], crossed[:, lanes]], axis=1)
        for lanes in (slice(0, half), slice(half, NX))
    ]
    flip = iota((size, NX), 1) % 2 == 0
    parts += [jnp.where(flip, part, -part) for part in parts]
    stacked = jnp.concatenate(parts, axis=0).astype(BF16)
    table_copy.wait()
    sums = dot_t(table_ref[...], stacked)
    even = iota((half, size), 0) % 2 == 0
    for upper in range(2):
        first = sums[:, 2 * upper * size : (2 * upper + 1) * size]
        second = sums[:, (2 * upper + 1) * size : (2 * upper + 2) * size]
        spectra = (first + jnp.where(even, second, -second)).astype(BF16)
        out_ref[upper * GX // 2 : (upper + 1) * GX // 2] = spectra.reshape(GX // 2, NXL, size)


def dft(lines):
    hbm = pl.BlockSpec(memory_space=pltpu.HBM)
    return pl.pallas_call(
        dft_kernel,
        out_shape=jax.ShapeDtypeStruct((GX, NXL, COILS * AL * 2), BF16),
        in_specs=[hbm, hbm],
        scratch_shapes=[
            pltpu.VMEM((COILS, 1, AL, 2, NX), BF16),
            pltpu.VMEM((NX // 2, NX), BF16),
            pltpu.SemaphoreType.DMA((2,)),
        ],
        compiler_params=room(62),
        name="dft",
    )(lines, dft_table())


def slab_kernel(in_ref, out_ref, rows_ref):
    rows_ref[...] = in_ref[...].reshape(GX * NXL, AL * SC).astype(F32)
    eye = column_onehot(iota((128, 1), 0), 128)
    group = 128 // GX
    k = iota((AL * 128, 1), 0)
    place = column_onehot((k % 128) // GX * NY3 + (k % GX) * AL + k // 128, group * NY3)
    flats = []
    for part in range(NXL // group):
        rows = jnp.concatenate(
            [rows_ref[pl.ds(part * group + x, GX, stride=NXL), :] for x in range(group)], axis=0
        ).astype(BF16)
        turned = dot_t(eye, rows).astype(BF16)
        flats.append(
            jnp.concatenate([turned[al * SC : (al + 1) * SC] for al in range(AL)], axis=1)
        )
    spread = dot(jnp.concatenate(flats, axis=0), place).astype(BF16)
    for part in range(NXL // group):
        for x in range(group):
            out_ref[part * group + x] = spread[
                part * SC : (part + 1) * SC, x * NY3 : (x + 1) * NY3
            ]


def to_slab(lines):
    return pl.pallas_call(
        slab_kernel,
        out_shape=jax.ShapeDtypeStruct((NXL, SC, NY3), BF16),
        scratch_shapes=[pltpu.VMEM((GX * NXL, AL * SC), F32)],
        compiler_params=room(8),
        name="slab",
    )(lines)


def weights_kernel(ky_ref, kz_ref, kernels_ref, out_ref, wide_ref, placed_ref):
    direct, crossed = [], []
    for t in range(6):
        for p in range(6):
            real, imag = kernels_ref[0, t, p], kernels_ref[1, t, p]
            direct += [real, imag]
            crossed += [(-imag.astype(F32)).astype(BF16), real]
    direct = jnp.concatenate(direct, axis=0)
    crossed = jnp.concatenate(crossed, axis=0)
    h = iota((2 * COILS, 1), 0)
    v, coil = h // COILS, h % COILS
    for odd in range(2):
        at = odd * 2 * SC + v * SC + coil
        plain = column_onehot(at, 4 * SC)
        swapped = column_onehot(at + COILS, 4 * SC).astype(F32)
        swapped = jnp.where(v == 0, swapped, -swapped).astype(BF16)
        wide = (dot(direct, plain) + dot(crossed, swapped)).astype(BF16)
        wide_ref[odd] = wide.reshape(36, SC, 4 * SC)
    b = lax.axis_index("kz")
    zero = jnp.zeros((SC, 4 * SC), BF16)
    for t in range(6):
        kz, ky = kz_ref[t], ky_ref[t]
        for pair in range(8):
            total = None
            for odd in range(2):
                q = 2 * pair + odd
                if q >= ROWS3 * SHIFTS:
                    continue
                row, shift = q // SHIFTS - 1, q % SHIFTS - 2
                j, i = row - kz, shift - ky
                used = (j >= 0) & (j < 2) & (i >= 0) & (i < 3)
                if row == -1:
                    used = used & (b > 0)
                if row == 1:
                    used = used & (b < NZC - 1)
                p = jnp.where(used, 3 * j + i, 0)
                block = jnp.where(used, wide_ref[odd, t * 6 + p], zero)
                total = block if total is None else total + block
            placed_ref[t // 2, (t % 2) * SC : (t % 2 + 1) * SC, pair * 4 * SC : (pair + 1) * 4 * SC] = total
    r = iota((2 * SC, 1), 0)
    weave = column_onehot((r % 2) * SC + r // 2, 2 * SC)
    for ry in range(3):
        out_ref[ry * 2 * SC : (ry + 1) * 2 * SC] = dot(weave, placed_ref[ry]).astype(BF16)
    out_ref[6 * SC :] = column_onehot((SHIFTS + 2) * 2 * SC + r // 2, KPAD)


def placed_weights(kernels, ky_start, kz_start):
    smem = pl.BlockSpec(memory_space=pltpu.SMEM)
    vmem = pl.BlockSpec(memory_space=pltpu.VMEM)
    return pl.pallas_call(
        weights_kernel,
        out_shape=jax.ShapeDtypeStruct((8 * SC, KPAD), BF16),
        in_specs=[smem, smem, vmem],
        scratch_shapes=[
            pltpu.VMEM((2, 36, SC, 4 * SC), BF16),
            pltpu.VMEM((3, 2 * SC, KPAD), BF16),
        ],
        cost_estimate=pl.CostEstimate(flops=100_000_000, bytes_accessed=4_000_000, transcendentals=0),
        compiler_params=room(12),
        name="weights",
    )(ky_start, kz_start, kernels.transpose(0, 1, 3, 2, 4))


def fill_kernel(
    own_ref, next0_ref, next1_ref, mirror_ref, near_ref, far_ref, weight_ref,
    acquired_ref, out_ref, source_ref,
):
    odd = lax.axis_index("kz") % 2
    k = iota((NY3, 1), 0)
    lane = iota((NY3, SHIFTS * NY3), 1)
    want = lane % NY3 + lane // NY3 - 2
    straight = onehot(k == want)
    mirrored = onehot(NY3 - 1 - k == want)

    def spread(slab, moves, v, row, first):
        count = slab.shape[0]
        moved = dot(slab.reshape(count * SC, NY3), moves).astype(BF16)
        for d in range(SHIFTS):
            at = ((row * SHIFTS + d) * 2 + v) * SC
            if not isinstance(row, int):
                at = pl.multiple_of(at, SC)
            for n in range(count):
                x = first + n
                source_ref[x // 2, pl.ds(at, SC), (x % 2) * NY3 : (x % 2 + 1) * NY3] = moved[
                    n * SC : (n + 1) * SC, d * NY3 : (d + 1) * NY3
                ]

    spread(own_ref[...], straight, 0, 1, 0)
    spread(next0_ref[...], straight, 0, 2 - 2 * odd, 0)
    spread(next1_ref[...], straight, 0, 2 * odd, 0)
    spread(mirror_ref[...], mirrored, 1, 1, 0)
    spread(near_ref[...], mirrored, 1, 2 * odd, 0)
    spread(far_ref[...], mirrored, 1, 2 - 2 * odd, 0)
    weights = weight_ref[:, :KDIM]
    acquired = acquired_ref[...]
    n = iota((3 * NY3, 1), 0)
    weave = column_onehot((n % NY3) * 3 + n // NY3, 3 * NY3)
    parity = iota((2 * SC, NY3), 0) % 2
    masks = [jnp.broadcast_to(acquired, (2 * SC, NY3)) == 2 * ry + parity for ry in range(3)]
    for pair in range(NXL // 2):
        result = dot(weights, source_ref[pair])
        for half in range(2):
            x = 2 * pair + half
            lanes = slice(half * NY3, (half + 1) * NY3)
            kept = result[6 * SC : 8 * SC, lanes]
            chosen = [
                jnp.where(masks[ry], kept, result[ry * 2 * SC : (ry + 1) * 2 * SC, lanes])
                for ry in range(3)
            ]
            line = jnp.concatenate(chosen, axis=1).astype(BF16)
            woven = dot(line, weave).astype(BF16)
            for s in range(2):
                out_ref[s, x] = woven[s * SC : (s + 1) * SC].reshape(COILS, 2, 3 * NY3)


def fill(slabs, weights, acquired_at):
    return pl.pallas_call(
        fill_kernel,
        out_shape=jax.ShapeDtypeStruct((2, NXL, COILS, 2, 3 * NY3), BF16),
        scratch_shapes=[pltpu.VMEM((NXL // 2, KDIM, 2 * NY3), BF16)],
        compiler_params=room(24),
        name="fill",
    )(*slabs, weights, acquired_at)


def local(kspace_lines, acquired_at, ky_start, kz_start, kernels):
    spectra = dft(kspace_lines)
    gathered = lax.all_to_all(spectra, "gx", split_axis=0, concat_axis=0, tiled=True)
    weights = placed_weights(kernels, ky_start, kz_start)
    own = to_slab(gathered)

    def fetch(values, source_of):
        pairs = [(source_of(b) % NZC, b) for b in range(NZC)]
        return lax.ppermute(values, "kz", pairs)

    next1 = fetch(own, lambda b: b - 1 + 2 * (b % 2))
    next0 = fetch(own, lambda b: b + 1 - 2 * (b % 2))
    near = fetch(own, lambda b: NZC - 2 * (b % 2) - b)
    mirror = fetch(own, lambda b: NZC - 1 - b)
    far = fetch(next1, lambda b: NZC - 3 + 4 * (b % 2) - b)
    return fill((own, next0, next1, mirror, near, far), weights, acquired_at)


def solution(mesh):
    placed = (P(None, "kz", "gx", None, None), P("kz", None), P(), P(), P())
    return jax.shard_map(
        local,
        mesh=mesh,
        in_specs=placed,
        out_specs=P(None, "gx", None, "kz", None),
        check_vma=False,
    )
```

```python
import math

import jax
import jax.numpy as jnp
import numpy as np
from jax import lax
from jax.experimental import pallas as pl
from jax.experimental.pallas import tpu as pltpu
from jax.sharding import PartitionSpec as P


COILS = 16
NX = 512
NZC = 16
NY3 = 128
GX = 32
AL = NY3 // GX
NXL = NX // GX
SC = 2 * COILS
SHIFTS = 5
ROWS3 = 3
KDIM = ROWS3 * SHIFTS * 2 * SC
KPAD = 1024
KFAR = SHIFTS * SC
FARPAD = 384
F32 = jnp.float32
BF16 = jnp.bfloat16


def dft_table():
    index = np.arange(NX // 2)
    angle = (index[:, None] * index[None, :] % NX) * (2.0 * math.pi / NX)
    table = np.concatenate([np.cos(angle), np.sin(angle)], axis=1) / math.sqrt(NX)
    return jnp.asarray(table.astype(np.float32)).astype(BF16)


def iota(shape, dim):
    return lax.broadcasted_iota(jnp.int32, shape, dim)


def onehot(condition):
    return jnp.where(condition, 1.0, 0.0).astype(BF16)


def dot(a, b):
    return lax.dot_general(a, b, (((1,), (0,)), ((), ())), preferred_element_type=F32)


def dot_t(a, b):
    return lax.dot_general(a, b, (((1,), (1,)), ((), ())), preferred_element_type=F32)


def room(mib):
    return pltpu.CompilerParams(vmem_limit_bytes=mib << 20)


def column_onehot(target, lanes):
    return onehot(target == iota((target.shape[0], lanes), 1))


def dft_kernel(lines_hbm, table_hbm, out_ref, lines_ref, table_ref, sems):
    lines_copy = pltpu.make_async_copy(lines_hbm, lines_ref, sems.at[0])
    table_copy = pltpu.make_async_copy(table_hbm, table_ref, sems.at[1])
    lines_copy.start()
    table_copy.start()
    size = COILS * AL * 2
    row = iota((size, 1), 0)
    al, s, c = row // SC, (row // COILS) % 2, row % COILS
    line = (c * AL + al) * 2
    same = column_onehot(line + s, size)
    cross = column_onehot(line + 1 - s, size).astype(F32)
    cross = jnp.where(s == 0, -cross, cross).astype(BF16)
    lines_copy.wait()
    lines = lines_ref[...].reshape(size, NX)
    direct = dot(same, lines)
    crossed = dot(cross, lines)
    half = NX // 2
    flip = iota((size, half), 1) % 2 == 0
    parts = [
        jnp.concatenate([direct[:, lanes], crossed[:, lanes]], axis=1)
        for lanes in (slice(0, half), slice(half, NX))
    ]
    flip = iota((size, NX), 1) % 2 == 0
    parts += [jnp.where(flip, part, -part) for part in parts]
    stacked = jnp.concatenate(parts, axis=0).astype(BF16)
    table_copy.wait()
    sums = dot_t(table_ref[...], stacked)
    even = iota((half, size), 0) % 2 == 0
    for upper in range(2):
        first = sums[:, 2 * upper * size : (2 * upper + 1) * size]
        second = sums[:, (2 * upper + 1) * size : (2 * upper + 2) * size]
        spectra = (first + jnp.where(even, second, -second)).astype(BF16)
        out_ref[upper * GX // 2 : (upper + 1) * GX // 2] = spectra.reshape(GX // 2, NXL, size)


def dft(lines):
    hbm = pl.BlockSpec(memory_space=pltpu.HBM)
    return pl.pallas_call(
        dft_kernel,
        out_shape=jax.ShapeDtypeStruct((GX, NXL, COILS * AL * 2), BF16),
        in_specs=[hbm, hbm],
        scratch_shapes=[
            pltpu.VMEM((COILS, 1, AL, 2, NX), BF16),
            pltpu.VMEM((NX // 2, NX), BF16),
            pltpu.SemaphoreType.DMA((2,)),
        ],
        compiler_params=room(62),
        name="dft",
    )(lines, dft_table())


def slab_kernel(in_ref, out_ref, rows_ref):
    rows_ref[...] = in_ref[...].reshape(GX * NXL, AL * SC).astype(F32)
    eye = column_onehot(iota((128, 1), 0), 128)
    group = 128 // GX
    k = iota((AL * 128, 1), 0)
    place = column_onehot((k % 128) // GX * NY3 + (k % GX) * AL + k // 128, group * NY3)
    flats = []
    for part in range(NXL // group):
        rows = jnp.concatenate(
            [rows_ref[pl.ds(part * group + x, GX, stride=NXL), :] for x in range(group)], axis=0
        ).astype(BF16)
        turned = dot_t(eye, rows).astype(BF16)
        flats.append(
            jnp.concatenate([turned[al * SC : (al + 1) * SC] for al in range(AL)], axis=1)
        )
    spread = dot(jnp.concatenate(flats, axis=0), place).astype(BF16)
    for part in range(NXL // group):
        for x in range(group):
            out_ref[part * group + x] = spread[
                part * SC : (part + 1) * SC, x * NY3 : (x + 1) * NY3
            ]


def to_slab(lines):
    return pl.pallas_call(
        slab_kernel,
        out_shape=jax.ShapeDtypeStruct((NXL, SC, NY3), BF16),
        scratch_shapes=[pltpu.VMEM((GX * NXL, AL * SC), F32)],
        compiler_params=room(8),
        name="slab",
    )(lines)


def weights_kernel(
    ky_ref, kz_ref, kernels_ref, out_ref, far_ref, wide_ref, placed_ref, placed_far_ref
):
    direct, crossed = [], []
    for t in range(6):
        for p in range(6):
            real, imag = kernels_ref[0, t, p], kernels_ref[1, t, p]
            direct += [real, imag]
            crossed += [(-imag.astype(F32)).astype(BF16), real]
    direct = jnp.concatenate(direct, axis=0)
    crossed = jnp.concatenate(crossed, axis=0)
    h = iota((2 * COILS, 1), 0)
    v, coil = h // COILS, h % COILS
    for odd in range(2):
        at = odd * 2 * SC + v * SC + coil
        plain = column_onehot(at, 4 * SC)
        swapped = column_onehot(at + COILS, 4 * SC).astype(F32)
        swapped = jnp.where(v == 0, swapped, -swapped).astype(BF16)
        wide = (dot(direct, plain) + dot(crossed, swapped)).astype(BF16)
        wide_ref[odd] = wide.reshape(36, SC, 4 * SC)
    b = lax.axis_index("kz")
    zero = jnp.zeros((SC, 4 * SC), BF16)

    def block(t, odd, row, shift):
        j, i = row - kz_ref[t], shift - 2 - ky_ref[t]
        used = (j >= 0) & (j < 2) & (i >= 0) & (i < 3) & (b + row >= 0) & (b + row < NZC)
        return jnp.where(used, wide_ref[odd, t * 6 + jnp.where(used, 3 * j + i, 0)], zero)

    far_row = 1 - 2 * (b % 2)
    for t in range(6):
        rows = slice((t % 2) * SC, (t % 2 + 1) * SC)
        for pair in range(8):
            lanes = slice(pair * 4 * SC, (pair + 1) * 4 * SC)
            total = block(t, 0, pair * 2 // SHIFTS - 1, pair * 2 % SHIFTS)
            if pair < 7:
                q = pair * 2 + 1
                total = total + block(t, 1, q // SHIFTS - 1, q % SHIFTS)
            placed_ref[t // 2, rows, lanes] = total
        for pair in range(3):
            lanes = slice(pair * 4 * SC, (pair + 1) * 4 * SC)
            total = block(t, 0, far_row, pair * 2)
            if pair < 2:
                total = total + block(t, 1, far_row, pair * 2 + 1)
            placed_far_ref[t // 2, rows, lanes] = total
    r = iota((2 * SC, 1), 0)
    weave = column_onehot((r % 2) * SC + r // 2, 2 * SC)
    k, lane = iota((FARPAD, 1), 0), iota((FARPAD, KFAR), 1)
    virtual = onehot(k == lane // SC * 2 * SC + SC + lane % SC)
    for ry in range(3):
        rows = slice(ry * 2 * SC, (ry + 1) * 2 * SC)
        out_ref[rows] = dot(weave, placed_ref[ry]).astype(BF16)
        far = dot(weave, placed_far_ref[ry]).astype(BF16)
        far_ref[rows] = dot(far, virtual).astype(BF16)
    out_ref[6 * SC :] = column_onehot((SHIFTS + 2) * 2 * SC + r // 2, KPAD)


def placed_weights(kernels, ky_start, kz_start):
    smem = pl.BlockSpec(memory_space=pltpu.SMEM)
    vmem = pl.BlockSpec(memory_space=pltpu.VMEM)
    return pl.pallas_call(
        weights_kernel,
        out_shape=(
            jax.ShapeDtypeStruct((8 * SC, KPAD), BF16),
            jax.ShapeDtypeStruct((6 * SC, KFAR), BF16),
        ),
        in_specs=[smem, smem, vmem],
        scratch_shapes=[
            pltpu.VMEM((2, 36, SC, 4 * SC), BF16),
            pltpu.VMEM((3, 2 * SC, KPAD), BF16),
            pltpu.VMEM((3, 2 * SC, FARPAD), BF16),
        ],
        cost_estimate=pl.CostEstimate(flops=100_000_000, bytes_accessed=4_000_000, transcendentals=0),
        compiler_params=room(12),
        name="weights",
    )(ky_start, kz_start, kernels.transpose(0, 1, 3, 2, 4))


def spread(source_ref, slab, mirrored, at_of):
    k = iota((NY3, 1), 0)
    lane = iota((NY3, SHIFTS * NY3), 1)
    want = lane % NY3 + lane // NY3 - 2
    moves = onehot((NY3 - 1 - k if mirrored else k) == want)
    moved = dot(slab.reshape(NXL * SC, NY3), moves).astype(BF16)
    for d in range(SHIFTS):
        for x in range(NXL):
            source_ref[x // 2, pl.ds(at_of(d), SC), (x % 2) * NY3 : (x % 2 + 1) * NY3] = moved[
                x * SC : (x + 1) * SC, d * NY3 : (d + 1) * NY3
            ]


def early_kernel(
    own_ref, next0_ref, next1_ref, mirror_ref, near_ref, weight_ref, sums_ref, source_ref
):
    odd = lax.axis_index("kz") % 2

    def at(row, v):
        return lambda d: pl.multiple_of(((row * SHIFTS + d) * 2 + v) * SC, SC)

    first, last = 2 * odd, 2 - 2 * odd
    for d in range(SHIFTS):
        for pair in range(NXL // 2):
            source_ref[pair, pl.ds(at(last, 1)(d), SC), :] = jnp.zeros((SC, 2 * NY3), BF16)
    spread(source_ref, own_ref[...], False, at(1, 0))
    spread(source_ref, next1_ref[...], False, at(first, 0))
    spread(source_ref, near_ref[...], True, at(first, 1))
    spread(source_ref, mirror_ref[...], True, at(1, 1))
    spread(source_ref, next0_ref[...], False, at(last, 0))
    weights = weight_ref[:, :KDIM]
    for pair in range(NXL // 2):
        sums_ref[pair] = dot(weights, source_ref[pair])


def early(slabs, weights):
    return pl.pallas_call(
        early_kernel,
        out_shape=jax.ShapeDtypeStruct((NXL // 2, 8 * SC, 2 * NY3), F32),
        scratch_shapes=[pltpu.VMEM((NXL // 2, KDIM, 2 * NY3), BF16)],
        compiler_params=room(16),
        cost_estimate=pl.CostEstimate(
            flops=1_500_000_000, bytes_accessed=4_000_000, transcendentals=0
        ),
        name="early",
    )(*slabs, weights)


def late_kernel(
    sums_ref, far_ref, weight_ref, acquired_ref, out_hbm, source_ref, out_ref, sems
):
    spread(source_ref, far_ref[...], True, lambda d: d * SC)
    weights = weight_ref[...]
    acquired = acquired_ref[...]
    n = iota((3 * NY3, 1), 0)
    weave = column_onehot((n % NY3) * 3 + n // NY3, 3 * NY3)
    parity = iota((2 * SC, NY3), 0) % 2
    masks = [jnp.broadcast_to(acquired, (2 * SC, NY3)) == 2 * ry + parity for ry in range(3)]
    copies = []
    for pair in range(NXL // 2):
        result = dot(weights, source_ref[pair]) + sums_ref[pair, : 6 * SC]
        lines = []
        for half in range(2):
            lanes = slice(half * NY3, (half + 1) * NY3)
            kept = sums_ref[pair, 6 * SC :, lanes]
            chosen = [
                jnp.where(masks[ry], kept, result[ry * 2 * SC : (ry + 1) * 2 * SC, lanes])
                for ry in range(3)
            ]
            lines.append(jnp.concatenate(chosen, axis=1).astype(BF16))
        woven = dot(jnp.concatenate(lines, axis=0), weave).astype(BF16)
        for half in range(2):
            for s in range(2):
                at = (half * 2 + s) * SC
                out_ref[s, 2 * pair + half] = woven[at : at + SC].reshape(COILS, 2, 3 * NY3)
        for s in range(2):
            two = pl.ds(2 * pair, 2)
            copy = pltpu.make_async_copy(out_ref.at[s, two], out_hbm.at[s, two], sems.at[s, pair])
            copy.start()
            copies.append(copy)
    for copy in copies:
        copy.wait()


def late(sums, far, weights, acquired_at):
    vmem = pl.BlockSpec(memory_space=pltpu.VMEM)
    shape = (2, NXL, COILS, 2, 3 * NY3)
    return pl.pallas_call(
        late_kernel,
        out_shape=jax.ShapeDtypeStruct(shape, BF16),
        in_specs=[vmem] * 4,
        out_specs=pl.BlockSpec(memory_space=pltpu.HBM),
        scratch_shapes=[
            pltpu.VMEM((NXL // 2, KFAR, 2 * NY3), BF16),
            pltpu.VMEM(shape, BF16),
            pltpu.SemaphoreType.DMA((2, NXL // 2)),
        ],
        compiler_params=room(16),
        name="late",
    )(sums, far, weights, acquired_at)


def local(kspace_lines, acquired_at, ky_start, kz_start, kernels):
    spectra = dft(kspace_lines)
    gathered = lax.all_to_all(spectra, "gx", split_axis=0, concat_axis=0, tiled=True)
    weights, far_weights = placed_weights(kernels, ky_start, kz_start)
    own = to_slab(gathered)

    def fetch(values, source_of):
        pairs = [(source_of(b) % NZC, b) for b in range(NZC)]
        return lax.ppermute(values, "kz", pairs)

    next1 = fetch(own, lambda b: b - 1 + 2 * (b % 2))
    next0 = fetch(own, lambda b: b + 1 - 2 * (b % 2))
    near = fetch(own, lambda b: NZC - 2 * (b % 2) - b)
    mirror = fetch(own, lambda b: NZC - 1 - b)
    far = fetch(next1, lambda b: NZC - 3 + 4 * (b % 2) - b)
    sums = early((own, next0, next1, mirror, near), weights)
    return late(sums, far, far_weights, acquired_at)


def solution(mesh):
    placed = (P(None, "kz", "gx", None, None), P("kz", None), P(), P(), P())
    return jax.shard_map(
        local,
        mesh=mesh,
        in_specs=placed,
        out_specs=P(None, "gx", None, "kz", None),
        check_vma=False,
    )
```

```python
import functools
import math

import jax
import jax.numpy as jnp
import numpy as np
from jax import lax
from jax.experimental import pallas as pl
from jax.experimental.pallas import tpu as pltpu
from jax.sharding import PartitionSpec as P


COILS = 16
NX = 512
NZC = 16
NY3 = 128
GX = 32
AL = NY3 // GX
NXL = NX // GX
SC = 2 * COILS
SHIFTS = 5
ROWS3 = 3
KDIM = ROWS3 * SHIFTS * 2 * SC
KPAD = 1024
KFAR = SHIFTS * SC
FARPAD = 384
F32 = jnp.float32
BF16 = jnp.bfloat16


def dft_table():
    index = np.arange(NX // 2)
    angle = (index[:, None] * index[None, :] % NX) * (2.0 * math.pi / NX)
    table = np.concatenate([np.cos(angle), np.sin(angle)], axis=1) / math.sqrt(NX)
    return jnp.asarray(table.astype(np.float32)).astype(BF16)


def iota(shape, dim):
    return lax.broadcasted_iota(jnp.int32, shape, dim)


def onehot(condition):
    return jnp.where(condition, 1.0, 0.0).astype(BF16)


def dot(a, b):
    return lax.dot_general(a, b, (((1,), (0,)), ((), ())), preferred_element_type=F32)


def dot_t(a, b):
    return lax.dot_general(a, b, (((1,), (1,)), ((), ())), preferred_element_type=F32)


def room(mib):
    return pltpu.CompilerParams(vmem_limit_bytes=mib << 20)


def column_onehot(target, lanes):
    return onehot(target == iota((target.shape[0], lanes), 1))


def dft_kernel(lines_hbm, table_hbm, out_ref, lines_ref, table_ref, sems):
    lines_copy = pltpu.make_async_copy(lines_hbm, lines_ref, sems.at[0])
    table_copy = pltpu.make_async_copy(table_hbm, table_ref, sems.at[1])
    lines_copy.start()
    table_copy.start()
    size = COILS * AL * 2
    row = iota((size, 1), 0)
    al, s, c = row // SC, (row // COILS) % 2, row % COILS
    line = (c * AL + al) * 2
    same = column_onehot(line + s, size)
    cross = column_onehot(line + 1 - s, size).astype(F32)
    cross = jnp.where(s == 0, -cross, cross).astype(BF16)
    lines_copy.wait()
    lines = lines_ref[...].reshape(size, NX)
    direct = dot(same, lines)
    crossed = dot(cross, lines)
    half = NX // 2
    flip = iota((size, half), 1) % 2 == 0
    parts = [
        jnp.concatenate([direct[:, lanes], crossed[:, lanes]], axis=1)
        for lanes in (slice(0, half), slice(half, NX))
    ]
    flip = iota((size, NX), 1) % 2 == 0
    parts += [jnp.where(flip, part, -part) for part in parts]
    stacked = jnp.concatenate(parts, axis=0).astype(BF16)
    table_copy.wait()
    sums = dot_t(table_ref[...], stacked)
    even = iota((half, size), 0) % 2 == 0
    for upper in range(2):
        first = sums[:, 2 * upper * size : (2 * upper + 1) * size]
        second = sums[:, (2 * upper + 1) * size : (2 * upper + 2) * size]
        spectra = (first + jnp.where(even, second, -second)).astype(BF16)
        out_ref[upper * GX // 2 : (upper + 1) * GX // 2] = spectra.reshape(GX // 2, NXL, size)


def dft(lines):
    hbm = pl.BlockSpec(memory_space=pltpu.HBM)
    return pl.pallas_call(
        dft_kernel,
        out_shape=jax.ShapeDtypeStruct((GX, NXL, COILS * AL * 2), BF16),
        in_specs=[hbm, hbm],
        scratch_shapes=[
            pltpu.VMEM((COILS, 1, AL, 2, NX), BF16),
            pltpu.VMEM((NX // 2, NX), BF16),
            pltpu.SemaphoreType.DMA((2,)),
        ],
        compiler_params=room(62),
        name="dft",
    )(lines, dft_table())


def slab_kernel(in_ref, place_ref, out_ref, rows_ref):
    rows_ref[...] = in_ref[...].reshape(GX * NXL, AL * SC).astype(F32)
    eye = column_onehot(iota((128, 1), 0), 128)
    group = 128 // GX
    flats = []
    for part in range(NXL // group):
        rows = jnp.concatenate(
            [rows_ref[pl.ds(part * group + x, GX, stride=NXL), :] for x in range(group)], axis=0
        ).astype(BF16)
        turned = dot_t(eye, rows).astype(BF16)
        flats.append(
            jnp.concatenate([turned[al * SC : (al + 1) * SC] for al in range(AL)], axis=1)
        )
    spread = dot(jnp.concatenate(flats, axis=0), place_ref[...]).astype(BF16)
    for part in range(NXL // group):
        for x in range(group):
            out_ref[part * group + x] = spread[
                part * SC : (part + 1) * SC, x * NY3 : (x + 1) * NY3
            ]


def to_slab(lines, place):
    return pl.pallas_call(
        slab_kernel,
        out_shape=jax.ShapeDtypeStruct((NXL, SC, NY3), BF16),
        scratch_shapes=[pltpu.VMEM((GX * NXL, AL * SC), F32)],
        compiler_params=room(8),
        name="slab",
    )(lines, place)


def make_tables(place_ref, moves_ref, weave_ref):
    group = 128 // GX
    k = iota((AL * 128, 1), 0)
    place_ref[...] = column_onehot(
        (k % 128) // GX * NY3 + (k % GX) * AL + k // 128, group * NY3
    )
    k = iota((NY3, 1), 0)
    for d in range(SHIFTS):
        lanes = slice(d * NY3, (d + 1) * NY3)
        moves_ref[0, :, lanes] = column_onehot(k - (d - 2), NY3)
        moves_ref[1, :, lanes] = column_onehot(NY3 - 1 - k - (d - 2), NY3)
    k = iota((3 * NY3, 1), 0)
    weave_ref[...] = column_onehot((k % NY3) * 3 + k // NY3, 3 * NY3)


def weights_kernel(
    ky_ref, kz_ref, kernels_ref, out_ref, far_ref, place_ref, moves_ref, weave_ref,
    wide_ref, placed_ref, placed_far_ref,
):
    make_tables(place_ref, moves_ref, weave_ref)
    direct, crossed = [], []
    for t in range(6):
        for p in range(6):
            real, imag = kernels_ref[0, t, p], kernels_ref[1, t, p]
            direct += [real, imag]
            crossed += [(-imag.astype(F32)).astype(BF16), real]
    direct = jnp.concatenate(direct, axis=0)
    crossed = jnp.concatenate(crossed, axis=0)
    h = iota((2 * COILS, 1), 0)
    v, coil = h // COILS, h % COILS
    for odd in range(2):
        at = odd * 2 * SC + v * SC + coil
        plain = column_onehot(at, 4 * SC)
        swapped = column_onehot(at + COILS, 4 * SC).astype(F32)
        swapped = jnp.where(v == 0, swapped, -swapped).astype(BF16)
        wide = (dot(direct, plain) + dot(crossed, swapped)).astype(BF16)
        wide_ref[odd] = wide.reshape(36, SC, 4 * SC)
    b = lax.axis_index("kz")
    zero = jnp.zeros((SC, 4 * SC), BF16)

    def block(t, odd, row, shift):
        j, i = row - kz_ref[t], shift - 2 - ky_ref[t]
        used = (j >= 0) & (j < 2) & (i >= 0) & (i < 3) & (b + row >= 0) & (b + row < NZC)
        return jnp.where(used, wide_ref[odd, t * 6 + jnp.where(used, 3 * j + i, 0)], zero)

    far_row = 1 - 2 * (b % 2)
    for t in range(6):
        rows = slice((t % 2) * SC, (t % 2 + 1) * SC)
        for pair in range(8):
            lanes = slice(pair * 4 * SC, (pair + 1) * 4 * SC)
            total = block(t, 0, pair * 2 // SHIFTS - 1, pair * 2 % SHIFTS)
            if pair < 7:
                q = pair * 2 + 1
                total = total + block(t, 1, q // SHIFTS - 1, q % SHIFTS)
            placed_ref[t // 2, rows, lanes] = total
        for pair in range(3):
            lanes = slice(pair * 4 * SC, (pair + 1) * 4 * SC)
            total = block(t, 0, far_row, pair * 2)
            if pair < 2:
                total = total + block(t, 1, far_row, pair * 2 + 1)
            placed_far_ref[t // 2, rows, lanes] = total
    r = iota((2 * SC, 1), 0)
    weave = column_onehot((r % 2) * SC + r // 2, 2 * SC)
    k, lane = iota((FARPAD, 1), 0), iota((FARPAD, KFAR), 1)
    virtual = onehot(k == lane // SC * 2 * SC + SC + lane % SC)
    for ry in range(3):
        rows = slice(ry * 2 * SC, (ry + 1) * 2 * SC)
        out_ref[rows] = dot(weave, placed_ref[ry]).astype(BF16)
        far = dot(weave, placed_far_ref[ry]).astype(BF16)
        far_ref[rows] = dot(far, virtual).astype(BF16)
    out_ref[6 * SC :] = column_onehot((SHIFTS + 2) * 2 * SC + r // 2, KPAD)


def placed_weights(kernels, ky_start, kz_start):
    smem = pl.BlockSpec(memory_space=pltpu.SMEM)
    vmem = pl.BlockSpec(memory_space=pltpu.VMEM)
    return pl.pallas_call(
        weights_kernel,
        out_shape=(
            jax.ShapeDtypeStruct((8 * SC, KPAD), BF16),
            jax.ShapeDtypeStruct((6 * SC, KFAR), BF16),
            jax.ShapeDtypeStruct((AL * 128, 128 // GX * NY3), BF16),
            jax.ShapeDtypeStruct((2, NY3, SHIFTS * NY3), BF16),
            jax.ShapeDtypeStruct((3 * NY3, 3 * NY3), BF16),
        ),
        in_specs=[smem, smem, vmem],
        scratch_shapes=[
            pltpu.VMEM((2, 36, SC, 4 * SC), BF16),
            pltpu.VMEM((3, 2 * SC, KPAD), BF16),
            pltpu.VMEM((3, 2 * SC, FARPAD), BF16),
        ],
        cost_estimate=pl.CostEstimate(flops=100_000_000, bytes_accessed=4_000_000, transcendentals=0),
        compiler_params=room(12),
        name="weights",
    )(ky_start, kz_start, kernels.transpose(0, 1, 3, 2, 4))


def spread(source_ref, slab, moves, at_of):
    count = slab.shape[0]
    moved = dot(slab.reshape(count * SC, NY3), moves).astype(BF16)
    for d in range(SHIFTS):
        for x in range(count):
            source_ref[x // 2, pl.ds(at_of(d), SC), (x % 2) * NY3 : (x % 2 + 1) * NY3] = moved[
                x * SC : (x + 1) * SC, d * NY3 : (d + 1) * NY3
            ]


def at(row, v):
    return lambda d: pl.multiple_of(((row * SHIFTS + d) * 2 + v) * SC, SC)


def early_kernel(own_ref, next0_ref, next1_ref, moves_ref, source_ref):
    odd = lax.axis_index("kz") % 2
    first, last = 2 * odd, 2 - 2 * odd
    for d in range(SHIFTS):
        for pair in range(NXL // 2):
            source_ref[pair, pl.ds(at(last, 1)(d), SC), :] = jnp.zeros((SC, 2 * NY3), BF16)
    spread(source_ref, own_ref[...], moves_ref[0], at(1, 0))
    spread(source_ref, next1_ref[...], moves_ref[0], at(first, 0))
    spread(source_ref, next0_ref[...], moves_ref[0], at(last, 0))


def middle_kernel(near_ref, weight_ref, moves_ref, _, sums_ref, source_ref):
    spread(source_ref, near_ref[0], moves_ref[1], at(2 * (lax.axis_index("kz") % 2), 1))
    spread(source_ref, near_ref[1], moves_ref[1], at(1, 1))
    weights = weight_ref[:, :KDIM]
    for pair in range(NXL // 2):
        sums_ref[pair] = dot(weights, source_ref[pair])


def early(slabs, near, weights, moves):
    vmem = pl.BlockSpec(memory_space=pltpu.VMEM)
    source = jax.ShapeDtypeStruct((NXL // 2, KDIM, 2 * NY3), BF16)
    spread_out = pl.pallas_call(
        early_kernel,
        out_shape=source,
        in_specs=[vmem] * 4,
        out_specs=vmem,
        compiler_params=room(12),
        cost_estimate=pl.CostEstimate(
            flops=500_000_000, bytes_accessed=4_000_000, transcendentals=0
        ),
        name="early",
    )(*slabs, moves)
    return pl.pallas_call(
        middle_kernel,
        out_shape=(jax.ShapeDtypeStruct((NXL // 2, 8 * SC, 2 * NY3), F32), source),
        in_specs=[vmem] * 4,
        out_specs=(vmem, vmem),
        input_output_aliases={3: 1},
        compiler_params=room(16),
        cost_estimate=pl.CostEstimate(
            flops=1_000_000_000, bytes_accessed=4_000_000, transcendentals=0
        ),
        name="middle",
    )(near, weights, moves, spread_out)[0]


def late_kernel(
    start, sums_ref, far_ref, weight_ref, moves_ref, weave_ref, acquired_ref, *rest
):
    out_hbm, source_ref, out_ref, sems = rest[-4:]
    spread(source_ref, far_ref[...], moves_ref[1], lambda d: d * SC)
    weights = weight_ref[...]
    acquired = acquired_ref[...]
    weave = weave_ref[...]
    parity = iota((2 * SC, NY3), 0) % 2
    masks = [jnp.broadcast_to(acquired, (2 * SC, NY3)) == 2 * ry + parity for ry in range(3)]
    copies = []
    for pair in range(NXL // 4):
        full = start + pair
        result = dot(weights, source_ref[pair]) + sums_ref[full, : 6 * SC]
        lines = []
        for half in range(2):
            lanes = slice(half * NY3, (half + 1) * NY3)
            kept = sums_ref[full, 6 * SC :, lanes]
            chosen = [
                jnp.where(masks[ry], kept, result[ry * 2 * SC : (ry + 1) * 2 * SC, lanes])
                for ry in range(3)
            ]
            lines.append(jnp.concatenate(chosen, axis=1).astype(BF16))
        woven = dot(jnp.concatenate(lines, axis=0), weave).astype(BF16)
        for half in range(2):
            for s in range(2):
                at = (half * 2 + s) * SC
                out_ref[s, 2 * pair + half] = woven[at : at + SC].reshape(COILS, 2, 3 * NY3)
        for s in range(2):
            copy = pltpu.make_async_copy(
                out_ref.at[s, pl.ds(2 * pair, 2)], out_hbm.at[s, pl.ds(2 * full, 2)], sems.at[s, pair]
            )
            copy.start()
            copies.append(copy)
    for copy in copies:
        copy.wait()


def late(half, filled, sums, far, weights, moves, weave, acquired_at):
    vmem = pl.BlockSpec(memory_space=pltpu.VMEM)
    hbm = pl.BlockSpec(memory_space=pltpu.HBM)
    shape = (2, NXL, COILS, 2, 3 * NY3)
    return pl.pallas_call(
        functools.partial(late_kernel, half * NXL // 4),
        out_shape=jax.ShapeDtypeStruct(shape, BF16),
        in_specs=[vmem] * 6 + [hbm] * len(filled),
        out_specs=hbm,
        input_output_aliases={6: 0} if filled else {},
        scratch_shapes=[
            pltpu.VMEM((NXL // 4, KFAR, 2 * NY3), BF16),
            pltpu.VMEM((2, NXL // 2, COILS, 2, 3 * NY3), BF16),
            pltpu.SemaphoreType.DMA((2, NXL // 4)),
        ],
        compiler_params=room(16),
    )(sums, far, weights, moves, weave, acquired_at, *filled)


def local(kspace_lines, acquired_at, ky_start, kz_start, kernels):
    spectra = dft(kspace_lines)
    gathered = lax.all_to_all(spectra, "gx", split_axis=0, concat_axis=0, tiled=True)
    weights, far_weights, place, moves, weave = placed_weights(
        kernels, ky_start, kz_start
    )
    own = to_slab(gathered, place)

    def fetch(values, source_of):
        pairs = [(source_of(b) % NZC, b) for b in range(NZC)]
        return lax.ppermute(values, "kz", pairs)

    next1 = fetch(own, lambda b: b - 1 + 2 * (b % 2))
    next0 = fetch(own, lambda b: b + 1 - 2 * (b % 2))
    near = fetch(jnp.stack([own, next1]), lambda b: NZC - 2 * (b % 2) - b)
    far0 = fetch(next1[: NXL // 2], lambda b: NZC - 3 + 4 * (b % 2) - b)
    far1 = fetch(next1[NXL // 2 :], lambda b: NZC - 3 + 4 * (b % 2) - b)
    sums = early((own, next0, next1), near, weights, moves)
    first = late(0, (), sums, far0, far_weights, moves, weave, acquired_at)
    return late(1, (first,), sums, far1, far_weights, moves, weave, acquired_at)


def solution(mesh):
    placed = (P(None, "kz", "gx", None, None), P("kz", None), P(), P(), P())
    return jax.shard_map(
        local,
        mesh=mesh,
        in_specs=placed,
        out_specs=P(None, "gx", None, "kz", None),
        check_vma=False,
    )
```

```python
import math

import jax
import jax.numpy as jnp
import numpy as np
from jax import lax
from jax.experimental import pallas as pl
from jax.experimental.pallas import tpu as pltpu
from jax.sharding import PartitionSpec as P


COILS = 16
NX = 512
NZC = 16
NY3 = 128
GX = 32
AL = NY3 // GX
NXL = NX // GX
SC = 2 * COILS
SHIFTS = 5
ROWS3 = 3
KDIM = ROWS3 * SHIFTS * 2 * SC
KPAD = 1024
KFAR = SHIFTS * SC
FARPAD = 384
F32 = jnp.float32
BF16 = jnp.bfloat16


def dft_table():
    index = np.arange(NX // 2)
    angle = (index[:, None] * index[None, :] % NX) * (2.0 * math.pi / NX)
    table = np.concatenate([np.cos(angle), np.sin(angle)], axis=1) / math.sqrt(NX)
    return jnp.asarray(table.astype(np.float32)).astype(BF16)


def iota(shape, dim):
    return lax.broadcasted_iota(jnp.int32, shape, dim)


def onehot(condition):
    return jnp.where(condition, 1.0, 0.0).astype(BF16)


def dot(a, b):
    return lax.dot_general(a, b, (((1,), (0,)), ((), ())), preferred_element_type=F32)


def dot_t(a, b):
    return lax.dot_general(a, b, (((1,), (1,)), ((), ())), preferred_element_type=F32)


def room(mib):
    return pltpu.CompilerParams(vmem_limit_bytes=mib << 20)


def column_onehot(target, lanes):
    return onehot(target == iota((target.shape[0], lanes), 1))


def dft_kernel(lines_hbm, table_hbm, out_ref, lines_ref, table_ref, sems):
    lines_copy = pltpu.make_async_copy(lines_hbm, lines_ref, sems.at[0])
    table_copy = pltpu.make_async_copy(table_hbm, table_ref, sems.at[1])
    lines_copy.start()
    table_copy.start()
    size = COILS * AL * 2
    row = iota((size, 1), 0)
    al, s, c = row // SC, (row // COILS) % 2, row % COILS
    line = (c * AL + al) * 2
    same = column_onehot(line + s, size)
    cross = column_onehot(line + 1 - s, size).astype(F32)
    cross = jnp.where(s == 0, -cross, cross).astype(BF16)
    lines_copy.wait()
    lines = lines_ref[...].reshape(size, NX)
    direct = dot(same, lines)
    crossed = dot(cross, lines)
    half = NX // 2
    flip = iota((size, half), 1) % 2 == 0
    parts = [
        jnp.concatenate([direct[:, lanes], crossed[:, lanes]], axis=1)
        for lanes in (slice(0, half), slice(half, NX))
    ]
    flip = iota((size, NX), 1) % 2 == 0
    parts += [jnp.where(flip, part, -part) for part in parts]
    stacked = jnp.concatenate(parts, axis=0).astype(BF16)
    table_copy.wait()
    sums = dot_t(table_ref[...], stacked)
    even = iota((half, size), 0) % 2 == 0
    for upper in range(2):
        first = sums[:, 2 * upper * size : (2 * upper + 1) * size]
        second = sums[:, (2 * upper + 1) * size : (2 * upper + 2) * size]
        spectra = (first + jnp.where(even, second, -second)).astype(BF16)
        out_ref[upper * GX // 2 : (upper + 1) * GX // 2] = spectra.reshape(GX // 2, NXL, size)


def dft(lines):
    hbm = pl.BlockSpec(memory_space=pltpu.HBM)
    return pl.pallas_call(
        dft_kernel,
        out_shape=jax.ShapeDtypeStruct((GX, NXL, COILS * AL * 2), BF16),
        in_specs=[hbm, hbm],
        scratch_shapes=[
            pltpu.VMEM((COILS, 1, AL, 2, NX), BF16),
            pltpu.VMEM((NX // 2, NX), BF16),
            pltpu.SemaphoreType.DMA((2,)),
        ],
        compiler_params=room(62),
        name="dft",
    )(lines, dft_table())


def slab_kernel(in_ref, place_ref, out_ref, rows_ref):
    rows_ref[...] = in_ref[...].reshape(GX * NXL, AL * SC).astype(F32)
    eye = column_onehot(iota((128, 1), 0), 128)
    group = 128 // GX
    flats = []
    for part in range(NXL // group):
        rows = jnp.concatenate(
            [rows_ref[pl.ds(part * group + x, GX, stride=NXL), :] for x in range(group)], axis=0
        ).astype(BF16)
        turned = dot_t(eye, rows).astype(BF16)
        flats.append(
            jnp.concatenate([turned[al * SC : (al + 1) * SC] for al in range(AL)], axis=1)
        )
    spread = dot(jnp.concatenate(flats, axis=0), place_ref[...]).astype(BF16)
    for part in range(NXL // group):
        for x in range(group):
            out_ref[part * group + x] = spread[
                part * SC : (part + 1) * SC, x * NY3 : (x + 1) * NY3
            ]


def to_slab(lines, place):
    return pl.pallas_call(
        slab_kernel,
        out_shape=jax.ShapeDtypeStruct((NXL, SC, NY3), BF16),
        scratch_shapes=[pltpu.VMEM((GX * NXL, AL * SC), F32)],
        compiler_params=room(8),
        name="slab",
    )(lines, place)


def make_tables(place_ref, moves_ref, weave_ref):
    group = 128 // GX
    k = iota((AL * 128, 1), 0)
    place_ref[...] = column_onehot(
        (k % 128) // GX * NY3 + (k % GX) * AL + k // 128, group * NY3
    )
    k = iota((NY3, 1), 0)
    for d in range(SHIFTS):
        lanes = slice(d * NY3, (d + 1) * NY3)
        moves_ref[0, :, lanes] = column_onehot(k - (d - 2), NY3)
        moves_ref[1, :, lanes] = column_onehot(NY3 - 1 - k - (d - 2), NY3)
    k = iota((3 * NY3, 1), 0)
    weave_ref[...] = column_onehot((k % NY3) * 3 + k // NY3, 3 * NY3)


def weights_kernel(
    ky_ref, kz_ref, kernels_ref, out_ref, far_ref, place_ref, moves_ref, weave_ref,
    wide_ref, placed_ref, placed_far_ref,
):
    make_tables(place_ref, moves_ref, weave_ref)
    direct, crossed = [], []
    for t in range(6):
        for p in range(6):
            real, imag = kernels_ref[0, t, p], kernels_ref[1, t, p]
            direct += [real, imag]
            crossed += [(-imag.astype(F32)).astype(BF16), real]
    direct = jnp.concatenate(direct, axis=0)
    crossed = jnp.concatenate(crossed, axis=0)
    h = iota((2 * COILS, 1), 0)
    v, coil = h // COILS, h % COILS
    for odd in range(2):
        at = odd * 2 * SC + v * SC + coil
        plain = column_onehot(at, 4 * SC)
        swapped = column_onehot(at + COILS, 4 * SC).astype(F32)
        swapped = jnp.where(v == 0, swapped, -swapped).astype(BF16)
        wide = (dot(direct, plain) + dot(crossed, swapped)).astype(BF16)
        wide_ref[odd] = wide.reshape(36, SC, 4 * SC)
    b = lax.axis_index("kz")
    zero = jnp.zeros((SC, 4 * SC), BF16)

    def block(t, odd, row, shift):
        j, i = row - kz_ref[t], shift - 2 - ky_ref[t]
        used = (j >= 0) & (j < 2) & (i >= 0) & (i < 3) & (b + row >= 0) & (b + row < NZC)
        return jnp.where(used, wide_ref[odd, t * 6 + jnp.where(used, 3 * j + i, 0)], zero)

    far_row = 1 - 2 * (b % 2)
    for t in range(6):
        rows = slice((t % 2) * SC, (t % 2 + 1) * SC)
        for pair in range(8):
            lanes = slice(pair * 4 * SC, (pair + 1) * 4 * SC)
            total = block(t, 0, pair * 2 // SHIFTS - 1, pair * 2 % SHIFTS)
            if pair < 7:
                q = pair * 2 + 1
                total = total + block(t, 1, q // SHIFTS - 1, q % SHIFTS)
            placed_ref[t // 2, rows, lanes] = total
        for pair in range(3):
            lanes = slice(pair * 4 * SC, (pair + 1) * 4 * SC)
            total = block(t, 0, far_row, pair * 2)
            if pair < 2:
                total = total + block(t, 1, far_row, pair * 2 + 1)
            placed_far_ref[t // 2, rows, lanes] = total
    r = iota((2 * SC, 1), 0)
    weave = column_onehot((r % 2) * SC + r // 2, 2 * SC)
    k, lane = iota((FARPAD, 1), 0), iota((FARPAD, KFAR), 1)
    virtual = onehot(k == lane // SC * 2 * SC + SC + lane % SC)
    for ry in range(3):
        rows = slice(ry * 2 * SC, (ry + 1) * 2 * SC)
        out_ref[rows] = dot(weave, placed_ref[ry]).astype(BF16)
        far = dot(weave, placed_far_ref[ry]).astype(BF16)
        far_ref[rows] = dot(far, virtual).astype(BF16)
    out_ref[6 * SC :] = column_onehot((SHIFTS + 2) * 2 * SC + r // 2, KPAD)


def placed_weights(kernels, ky_start, kz_start):
    smem = pl.BlockSpec(memory_space=pltpu.SMEM)
    vmem = pl.BlockSpec(memory_space=pltpu.VMEM)
    return pl.pallas_call(
        weights_kernel,
        out_shape=(
            jax.ShapeDtypeStruct((8 * SC, KPAD), BF16),
            jax.ShapeDtypeStruct((6 * SC, KFAR), BF16),
            jax.ShapeDtypeStruct((AL * 128, 128 // GX * NY3), BF16),
            jax.ShapeDtypeStruct((2, NY3, SHIFTS * NY3), BF16),
            jax.ShapeDtypeStruct((3 * NY3, 3 * NY3), BF16),
        ),
        in_specs=[smem, smem, vmem],
        scratch_shapes=[
            pltpu.VMEM((2, 36, SC, 4 * SC), BF16),
            pltpu.VMEM((3, 2 * SC, KPAD), BF16),
            pltpu.VMEM((3, 2 * SC, FARPAD), BF16),
        ],
        cost_estimate=pl.CostEstimate(flops=100_000_000, bytes_accessed=4_000_000, transcendentals=0),
        compiler_params=room(12),
        name="weights",
    )(ky_start, kz_start, kernels.transpose(0, 1, 3, 2, 4))


def spread(source_ref, slab, moves, at_of):
    moved = dot(slab.reshape(NXL * SC, NY3), moves).astype(BF16)
    for d in range(SHIFTS):
        for x in range(NXL):
            source_ref[x // 2, pl.ds(at_of(d), SC), (x % 2) * NY3 : (x % 2 + 1) * NY3] = moved[
                x * SC : (x + 1) * SC, d * NY3 : (d + 1) * NY3
            ]


def early_kernel(
    own_ref, next0_ref, next1_ref, mirror_ref, near_ref, weight_ref, moves_ref, sums_ref,
    source_ref,
):
    straight, mirrored = moves_ref[0], moves_ref[1]
    odd = lax.axis_index("kz") % 2

    def at(row, v):
        return lambda d: pl.multiple_of(((row * SHIFTS + d) * 2 + v) * SC, SC)

    first, last = 2 * odd, 2 - 2 * odd
    for d in range(SHIFTS):
        for pair in range(NXL // 2):
            source_ref[pair, pl.ds(at(last, 1)(d), SC), :] = jnp.zeros((SC, 2 * NY3), BF16)
    spread(source_ref, own_ref[...], straight, at(1, 0))
    spread(source_ref, next1_ref[...], straight, at(first, 0))
    spread(source_ref, near_ref[...], mirrored, at(first, 1))
    spread(source_ref, mirror_ref[...], mirrored, at(1, 1))
    spread(source_ref, next0_ref[...], straight, at(last, 0))
    weights = weight_ref[:, :KDIM]
    for pair in range(NXL // 2):
        sums_ref[pair] = dot(weights, source_ref[pair])


def early(slabs, weights, moves):
    return pl.pallas_call(
        early_kernel,
        out_shape=jax.ShapeDtypeStruct((NXL // 2, 8 * SC, 2 * NY3), F32),
        scratch_shapes=[pltpu.VMEM((NXL // 2, KDIM, 2 * NY3), BF16)],
        compiler_params=room(16),
        cost_estimate=pl.CostEstimate(
            flops=1_500_000_000, bytes_accessed=4_000_000, transcendentals=0
        ),
        name="early",
    )(*slabs, weights, moves)


def late_kernel(
    sums_ref, far_ref, weight_ref, moves_ref, weave_ref, acquired_ref, out_hbm,
    source_ref, out_ref, sems,
):
    spread(source_ref, far_ref[...], moves_ref[1], lambda d: d * SC)
    weights = weight_ref[...]
    acquired = acquired_ref[...]
    weave = weave_ref[...]
    parity = iota((2 * SC, NY3), 0) % 2
    masks = [jnp.broadcast_to(acquired, (2 * SC, NY3)) == 2 * ry + parity for ry in range(3)]
    copies = []
    for pair in range(NXL // 2):
        result = dot(weights, source_ref[pair]) + sums_ref[pair, : 6 * SC]
        lines = []
        for half in range(2):
            lanes = slice(half * NY3, (half + 1) * NY3)
            kept = sums_ref[pair, 6 * SC :, lanes]
            chosen = [
                jnp.where(masks[ry], kept, result[ry * 2 * SC : (ry + 1) * 2 * SC, lanes])
                for ry in range(3)
            ]
            lines.append(jnp.concatenate(chosen, axis=1).astype(BF16))
        woven = dot(jnp.concatenate(lines, axis=0), weave).astype(BF16)
        for half in range(2):
            for s in range(2):
                at = (half * 2 + s) * SC
                out_ref[s, 2 * pair + half] = woven[at : at + SC].reshape(COILS, 2, 3 * NY3)
        for s in range(2):
            two = pl.ds(2 * pair, 2)
            copy = pltpu.make_async_copy(out_ref.at[s, two], out_hbm.at[s, two], sems.at[s, pair])
            copy.start()
            copies.append(copy)
    for copy in copies:
        copy.wait()


def late(sums, far, weights, moves, weave, acquired_at):
    vmem = pl.BlockSpec(memory_space=pltpu.VMEM)
    shape = (2, NXL, COILS, 2, 3 * NY3)
    return pl.pallas_call(
        late_kernel,
        out_shape=jax.ShapeDtypeStruct(shape, BF16),
        in_specs=[vmem] * 6,
        out_specs=pl.BlockSpec(memory_space=pltpu.HBM),
        scratch_shapes=[
            pltpu.VMEM((NXL // 2, KFAR, 2 * NY3), BF16),
            pltpu.VMEM(shape, BF16),
            pltpu.SemaphoreType.DMA((2, NXL // 2)),
        ],
        compiler_params=room(16),
        name="late",
    )(sums, far, weights, moves, weave, acquired_at)


def local(kspace_lines, acquired_at, ky_start, kz_start, kernels):
    spectra = dft(kspace_lines)
    gathered = lax.all_to_all(spectra, "gx", split_axis=0, concat_axis=0, tiled=True)
    weights, far_weights, place, moves, weave = placed_weights(
        kernels, ky_start, kz_start
    )
    own = to_slab(gathered, place)

    def fetch(values, source_of):
        pairs = [(source_of(b) % NZC, b) for b in range(NZC)]
        return lax.ppermute(values, "kz", pairs)

    next1 = fetch(own, lambda b: b - 1 + 2 * (b % 2))
    next0 = fetch(own, lambda b: b + 1 - 2 * (b % 2))
    near = fetch(own, lambda b: NZC - 2 * (b % 2) - b)
    mirror = fetch(own, lambda b: NZC - 1 - b)
    far = fetch(next1, lambda b: NZC - 3 + 4 * (b % 2) - b)
    sums = early((own, next0, next1, mirror, near), weights, moves)
    return late(sums, far, far_weights, moves, weave, acquired_at)


def solution(mesh):
    placed = (P(None, "kz", "gx", None, None), P("kz", None), P(), P(), P())
    return jax.shard_map(
        local,
        mesh=mesh,
        in_specs=placed,
        out_specs=P(None, "gx", None, "kz", None),
        check_vma=False,
    )
```

```python
import functools
import math

import jax
import jax.numpy as jnp
import numpy as np
from jax import lax
from jax.experimental import pallas as pl
from jax.experimental.pallas import tpu as pltpu
from jax.sharding import PartitionSpec as P


COILS = 16
NX = 512
NZC = 16
NY3 = 128
GX = 32
AL = NY3 // GX
NXL = NX // GX
SC = 2 * COILS
SHIFTS = 5
ROWS3 = 3
KDIM = ROWS3 * SHIFTS * 2 * SC
KPAD = 1024
KFAR = SHIFTS * SC
FARPAD = 384
F32 = jnp.float32
BF16 = jnp.bfloat16


def dft_table():
    index = np.arange(NX // 2)
    angle = (index[:, None] * index[None, :] % NX) * (2.0 * math.pi / NX)
    table = np.concatenate([np.cos(angle), np.sin(angle)], axis=1) / math.sqrt(NX)
    return jnp.asarray(table.astype(np.float32)).astype(BF16)


def iota(shape, dim):
    return lax.broadcasted_iota(jnp.int32, shape, dim)


def onehot(condition):
    return jnp.where(condition, 1.0, 0.0).astype(BF16)


def dot(a, b):
    return lax.dot_general(a, b, (((1,), (0,)), ((), ())), preferred_element_type=F32)


def dot_t(a, b):
    return lax.dot_general(a, b, (((1,), (1,)), ((), ())), preferred_element_type=F32)


def room(mib):
    return pltpu.CompilerParams(vmem_limit_bytes=mib << 20)


def column_onehot(target, lanes):
    return onehot(target == iota((target.shape[0], lanes), 1))


def dft_kernel(lines_hbm, table_hbm, out_ref, lines_ref, table_ref, sems):
    lines_copy = pltpu.make_async_copy(lines_hbm, lines_ref, sems.at[0])
    table_copy = pltpu.make_async_copy(table_hbm, table_ref, sems.at[1])
    lines_copy.start()
    table_copy.start()
    size = COILS * AL * 2
    row = iota((size, 1), 0)
    al, s, c = row // SC, (row // COILS) % 2, row % COILS
    line = (c * AL + al) * 2
    same = column_onehot(line + s, size)
    cross = column_onehot(line + 1 - s, size).astype(F32)
    cross = jnp.where(s == 0, -cross, cross).astype(BF16)
    lines_copy.wait()
    lines = lines_ref[...].reshape(size, NX)
    direct = dot(same, lines)
    crossed = dot(cross, lines)
    half = NX // 2
    flip = iota((size, half), 1) % 2 == 0
    parts = [
        jnp.concatenate([direct[:, lanes], crossed[:, lanes]], axis=1)
        for lanes in (slice(0, half), slice(half, NX))
    ]
    flip = iota((size, NX), 1) % 2 == 0
    parts += [jnp.where(flip, part, -part) for part in parts]
    stacked = jnp.concatenate(parts, axis=0).astype(BF16)
    table_copy.wait()
    sums = dot_t(table_ref[...], stacked)
    even = iota((half, size), 0) % 2 == 0
    for upper in range(2):
        first = sums[:, 2 * upper * size : (2 * upper + 1) * size]
        second = sums[:, (2 * upper + 1) * size : (2 * upper + 2) * size]
        spectra = (first + jnp.where(even, second, -second)).astype(BF16)
        out_ref[upper * GX // 2 : (upper + 1) * GX // 2] = spectra.reshape(GX // 2, NXL, size)


def dft(lines):
    hbm = pl.BlockSpec(memory_space=pltpu.HBM)
    return pl.pallas_call(
        dft_kernel,
        out_shape=jax.ShapeDtypeStruct((GX, NXL, COILS * AL * 2), BF16),
        in_specs=[hbm, hbm],
        scratch_shapes=[
            pltpu.VMEM((COILS, 1, AL, 2, NX), BF16),
            pltpu.VMEM((NX // 2, NX), BF16),
            pltpu.SemaphoreType.DMA((2,)),
        ],
        compiler_params=room(62),
        name="dft",
    )(lines, dft_table())


def slab_kernel(in_ref, place_ref, out_ref, rows_ref):
    rows_ref[...] = in_ref[...].reshape(GX * NXL, AL * SC).astype(F32)
    eye = column_onehot(iota((128, 1), 0), 128)
    group = 128 // GX
    flats = []
    for part in range(NXL // group):
        rows = jnp.concatenate(
            [rows_ref[pl.ds(part * group + x, GX, stride=NXL), :] for x in range(group)], axis=0
        ).astype(BF16)
        turned = dot_t(eye, rows).astype(BF16)
        flats.append(
            jnp.concatenate([turned[al * SC : (al + 1) * SC] for al in range(AL)], axis=1)
        )
    spread = dot(jnp.concatenate(flats, axis=0), place_ref[...]).astype(BF16)
    for part in range(NXL // group):
        for x in range(group):
            out_ref[part * group + x] = spread[
                part * SC : (part + 1) * SC, x * NY3 : (x + 1) * NY3
            ]


def to_slab(lines, place):
    return pl.pallas_call(
        slab_kernel,
        out_shape=jax.ShapeDtypeStruct((NXL, SC, NY3), BF16),
        scratch_shapes=[pltpu.VMEM((GX * NXL, AL * SC), F32)],
        compiler_params=room(8),
        name="slab",
    )(lines, place)


def make_tables(place_ref, moves_ref, weave_ref):
    group = 128 // GX
    k = iota((AL * 128, 1), 0)
    place_ref[...] = column_onehot(
        (k % 128) // GX * NY3 + (k % GX) * AL + k // 128, group * NY3
    )
    k = iota((NY3, 1), 0)
    for d in range(SHIFTS):
        lanes = slice(d * NY3, (d + 1) * NY3)
        moves_ref[0, :, lanes] = column_onehot(k - (d - 2), NY3)
        moves_ref[1, :, lanes] = column_onehot(NY3 - 1 - k - (d - 2), NY3)
    k = iota((3 * NY3, 1), 0)
    weave_ref[...] = column_onehot((k % NY3) * 3 + k // NY3, 3 * NY3)


def weights_kernel(
    ky_ref, kz_ref, kernels_ref, out_ref, far_ref, place_ref, moves_ref, weave_ref,
    wide_ref, placed_ref, placed_far_ref,
):
    make_tables(place_ref, moves_ref, weave_ref)
    direct, crossed = [], []
    for t in range(6):
        for p in range(6):
            real, imag = kernels_ref[0, t, p], kernels_ref[1, t, p]
            direct += [real, imag]
            crossed += [(-imag.astype(F32)).astype(BF16), real]
    direct = jnp.concatenate(direct, axis=0)
    crossed = jnp.concatenate(crossed, axis=0)
    h = iota((2 * COILS, 1), 0)
    v, coil = h // COILS, h % COILS
    for odd in range(2):
        at = odd * 2 * SC + v * SC + coil
        plain = column_onehot(at, 4 * SC)
        swapped = column_onehot(at + COILS, 4 * SC).astype(F32)
        swapped = jnp.where(v == 0, swapped, -swapped).astype(BF16)
        wide = (dot(direct, plain) + dot(crossed, swapped)).astype(BF16)
        wide_ref[odd] = wide.reshape(36, SC, 4 * SC)
    b = lax.axis_index("kz")
    zero = jnp.zeros((SC, 4 * SC), BF16)

    def block(t, odd, row, shift):
        j, i = row - kz_ref[t], shift - 2 - ky_ref[t]
        used = (j >= 0) & (j < 2) & (i >= 0) & (i < 3) & (b + row >= 0) & (b + row < NZC)
        return jnp.where(used, wide_ref[odd, t * 6 + jnp.where(used, 3 * j + i, 0)], zero)

    far_row = 1 - 2 * (b % 2)
    for t in range(6):
        rows = slice((t % 2) * SC, (t % 2 + 1) * SC)
        for pair in range(8):
            lanes = slice(pair * 4 * SC, (pair + 1) * 4 * SC)
            total = block(t, 0, pair * 2 // SHIFTS - 1, pair * 2 % SHIFTS)
            if pair < 7:
                q = pair * 2 + 1
                total = total + block(t, 1, q // SHIFTS - 1, q % SHIFTS)
            placed_ref[t // 2, rows, lanes] = total
        for pair in range(3):
            lanes = slice(pair * 4 * SC, (pair + 1) * 4 * SC)
            total = block(t, 0, far_row, pair * 2)
            if pair < 2:
                total = total + block(t, 1, far_row, pair * 2 + 1)
            placed_far_ref[t // 2, rows, lanes] = total
    r = iota((2 * SC, 1), 0)
    weave = column_onehot((r % 2) * SC + r // 2, 2 * SC)
    k, lane = iota((FARPAD, 1), 0), iota((FARPAD, KFAR), 1)
    virtual = onehot(k == lane // SC * 2 * SC + SC + lane % SC)
    for ry in range(3):
        rows = slice(ry * 2 * SC, (ry + 1) * 2 * SC)
        out_ref[rows] = dot(weave, placed_ref[ry]).astype(BF16)
        far = dot(weave, placed_far_ref[ry]).astype(BF16)
        far_ref[rows] = dot(far, virtual).astype(BF16)
    out_ref[6 * SC :] = column_onehot((SHIFTS + 2) * 2 * SC + r // 2, KPAD)


def placed_weights(kernels, ky_start, kz_start):
    smem = pl.BlockSpec(memory_space=pltpu.SMEM)
    vmem = pl.BlockSpec(memory_space=pltpu.VMEM)
    return pl.pallas_call(
        weights_kernel,
        out_shape=(
            jax.ShapeDtypeStruct((8 * SC, KPAD), BF16),
            jax.ShapeDtypeStruct((6 * SC, KFAR), BF16),
            jax.ShapeDtypeStruct((AL * 128, 128 // GX * NY3), BF16),
            jax.ShapeDtypeStruct((2, NY3, SHIFTS * NY3), BF16),
            jax.ShapeDtypeStruct((3 * NY3, 3 * NY3), BF16),
        ),
        in_specs=[smem, smem, vmem],
        scratch_shapes=[
            pltpu.VMEM((2, 36, SC, 4 * SC), BF16),
            pltpu.VMEM((3, 2 * SC, KPAD), BF16),
            pltpu.VMEM((3, 2 * SC, FARPAD), BF16),
        ],
        cost_estimate=pl.CostEstimate(flops=100_000_000, bytes_accessed=4_000_000, transcendentals=0),
        compiler_params=room(12),
        name="weights",
    )(ky_start, kz_start, kernels.transpose(0, 1, 3, 2, 4))


def spread(source_ref, slab, moves, at_of):
    count = slab.shape[0]
    moved = dot(slab.reshape(count * SC, NY3), moves).astype(BF16)
    for d in range(SHIFTS):
        for x in range(count):
            source_ref[x // 2, pl.ds(at_of(d), SC), (x % 2) * NY3 : (x % 2 + 1) * NY3] = moved[
                x * SC : (x + 1) * SC, d * NY3 : (d + 1) * NY3
            ]


def early_kernel(
    own_ref, next0_ref, next1_ref, near_ref, weight_ref, moves_ref, sums_ref,
    source_ref,
):
    straight, mirrored = moves_ref[0], moves_ref[1]
    odd = lax.axis_index("kz") % 2

    def at(row, v):
        return lambda d: pl.multiple_of(((row * SHIFTS + d) * 2 + v) * SC, SC)

    first, last = 2 * odd, 2 - 2 * odd
    for d in range(SHIFTS):
        for pair in range(NXL // 2):
            source_ref[pair, pl.ds(at(last, 1)(d), SC), :] = jnp.zeros((SC, 2 * NY3), BF16)
    spread(source_ref, own_ref[...], straight, at(1, 0))
    spread(source_ref, next1_ref[...], straight, at(first, 0))
    spread(source_ref, near_ref[0], mirrored, at(first, 1))
    spread(source_ref, near_ref[1], mirrored, at(1, 1))
    spread(source_ref, next0_ref[...], straight, at(last, 0))
    weights = weight_ref[:, :KDIM]
    for pair in range(NXL // 2):
        sums_ref[pair] = dot(weights, source_ref[pair])


def early(slabs, weights, moves):
    return pl.pallas_call(
        early_kernel,
        out_shape=jax.ShapeDtypeStruct((NXL // 2, 8 * SC, 2 * NY3), F32),
        scratch_shapes=[pltpu.VMEM((NXL // 2, KDIM, 2 * NY3), BF16)],
        compiler_params=room(16),
        cost_estimate=pl.CostEstimate(
            flops=1_500_000_000, bytes_accessed=4_000_000, transcendentals=0
        ),
        name="early",
    )(*slabs, weights, moves)


def late_kernel(
    start, sums_ref, far_ref, weight_ref, moves_ref, weave_ref, acquired_ref, *rest
):
    out_hbm, source_ref, out_ref, sems = rest[-4:]
    spread(source_ref, far_ref[...], moves_ref[1], lambda d: d * SC)
    weights = weight_ref[...]
    acquired = acquired_ref[...]
    weave = weave_ref[...]
    parity = iota((2 * SC, NY3), 0) % 2
    masks = [jnp.broadcast_to(acquired, (2 * SC, NY3)) == 2 * ry + parity for ry in range(3)]
    copies = []
    for pair in range(NXL // 4):
        full = start + pair
        result = dot(weights, source_ref[pair]) + sums_ref[full, : 6 * SC]
        lines = []
        for half in range(2):
            lanes = slice(half * NY3, (half + 1) * NY3)
            kept = sums_ref[full, 6 * SC :, lanes]
            chosen = [
                jnp.where(masks[ry], kept, result[ry * 2 * SC : (ry + 1) * 2 * SC, lanes])
                for ry in range(3)
            ]
            lines.append(jnp.concatenate(chosen, axis=1).astype(BF16))
        woven = dot(jnp.concatenate(lines, axis=0), weave).astype(BF16)
        for half in range(2):
            for s in range(2):
                at = (half * 2 + s) * SC
                out_ref[s, 2 * pair + half] = woven[at : at + SC].reshape(COILS, 2, 3 * NY3)
        for s in range(2):
            copy = pltpu.make_async_copy(
                out_ref.at[s, pl.ds(2 * pair, 2)], out_hbm.at[s, pl.ds(2 * full, 2)], sems.at[s, pair]
            )
            copy.start()
            copies.append(copy)
    for copy in copies:
        copy.wait()


def late(half, filled, sums, far, weights, moves, weave, acquired_at):
    vmem = pl.BlockSpec(memory_space=pltpu.VMEM)
    hbm = pl.BlockSpec(memory_space=pltpu.HBM)
    shape = (2, NXL, COILS, 2, 3 * NY3)
    return pl.pallas_call(
        functools.partial(late_kernel, half * NXL // 4),
        out_shape=jax.ShapeDtypeStruct(shape, BF16),
        in_specs=[vmem] * 6 + [hbm] * len(filled),
        out_specs=hbm,
        input_output_aliases={6: 0} if filled else {},
        scratch_shapes=[
            pltpu.VMEM((NXL // 4, KFAR, 2 * NY3), BF16),
            pltpu.VMEM((2, NXL // 2, COILS, 2, 3 * NY3), BF16),
            pltpu.SemaphoreType.DMA((2, NXL // 4)),
        ],
        compiler_params=room(16),
    )(sums, far, weights, moves, weave, acquired_at, *filled)


def local(kspace_lines, acquired_at, ky_start, kz_start, kernels):
    spectra = dft(kspace_lines)
    gathered = lax.all_to_all(spectra, "gx", split_axis=0, concat_axis=0, tiled=True)
    weights, far_weights, place, moves, weave = placed_weights(
        kernels, ky_start, kz_start
    )
    own = to_slab(gathered, place)

    def fetch(values, source_of):
        pairs = [(source_of(b) % NZC, b) for b in range(NZC)]
        return lax.ppermute(values, "kz", pairs)

    next1 = fetch(own, lambda b: b - 1 + 2 * (b % 2))
    next0 = fetch(own, lambda b: b + 1 - 2 * (b % 2))
    near = fetch(jnp.stack([own, next1]), lambda b: NZC - 2 * (b % 2) - b)
    far0 = fetch(next1[: NXL // 2], lambda b: NZC - 3 + 4 * (b % 2) - b)
    far1 = fetch(next1[NXL // 2 :], lambda b: NZC - 3 + 4 * (b % 2) - b)
    sums = early((own, next0, next1, near), weights, moves)
    first = late(0, (), sums, far0, far_weights, moves, weave, acquired_at)
    return late(1, (first,), sums, far1, far_weights, moves, weave, acquired_at)


def solution(mesh):
    placed = (P(None, "kz", "gx", None, None), P("kz", None), P(), P(), P())
    return jax.shard_map(
        local,
        mesh=mesh,
        in_specs=placed,
        out_specs=P(None, "gx", None, "kz", None),
        check_vma=False,
    )
```
